512 devices in a mesh: freq: 8 (over z_hi, core), tile: 64 (over y, z_lo, x).
Axes of the slice: x: 4, y: 8, z: 8 (z_hi: 4, z_lo: 2; z = z_hi * 2 + z_lo), core: 2. Of those that a mesh axis runs over, the one named last changes fastest.
Arguments:
- spectra: bfloat16 [2, 128, 256, 8192], P(None, None, 'freq', 'tile'), may hold values from -450 to 450
- seg_mask: int32 [128, 8192], P(None, 'tile'), may hold values 0 or 1
Outputs:
- coherence: bfloat16 [64, 2, 256, 128, 128], P('tile', None, None, 'freq')
The draws below stay inside these ranges and needn't reach their ends.
All inputs are finite; a program needn't handle non-finite values. No bound on the sum of `seg_mask` on one device may be relied on, other than what follows from the above.
Results may differ from the reference program's by a relative error of at most 0.012.
The reference program's roundings to bfloat16 on the way count: a program that leaves them out, or rounds other values in their place, can miss the bound.
Values may be sent and summed in bfloat16 or wider, within the bound.
A program may use at most 64 MiB of HBM per device.

```python
import math
import jax
import jax.numpy as jnp
from jax import lax

BLK = 128
F = 256
SEG = 128
LAGS = 512
CH = 8192
N_TILE = 64


def draw_spectra(key, part):
    key_base = jax.random.fold_in(key, 0)
    key_rough = jax.random.fold_in(key, 2)
    key_chan = jax.random.fold_in(key, 3)
    freq_pos = jnp.arange(F, dtype=jnp.float32) / (F - 1)
    base = jax.random.truncated_normal(key_base, -4.0, 4.0, (2, SEG, F, CH), jnp.float32)
    rough = jnp.exp(jax.random.uniform(key_rough, (F,), jnp.float32, -0.5, 0.5))
    freq_scale = jnp.power(10.0, freq_pos) * rough
    chan_scale = jnp.exp(jax.random.uniform(key_chan, (CH,), jnp.float32, 0.0, math.log(3.0)))
    return (base * freq_scale[None, None, :, None] * chan_scale[None, None, None, :]).astype(jnp.bfloat16)


def place_ends(result, rng, least, largest):
    longest = result.shape.index(max(result.shape))
    spots = []
    for shift in (0, 1):
        where = [jax.random.randint(jax.random.fold_in(rng, axis), (), 0, length) for axis, length in enumerate(result.shape)]
        where[longest] = (where[longest] + shift) % result.shape[longest]
        spots.append(tuple(where))
    return result.at[spots[0]].set(least).at[spots[1]].set(largest)


def setup_inputs(seed: int = 0) -> dict:
    arg_keys = jax.random.split(jax.random.key(seed), 3)
    return {
        "spectra": draw_spectra(jax.random.fold_in(arg_keys[2], 71), 0),
        "seg_mask": place_ends((jax.random.randint(arg_keys[1], (SEG, CH), 0, 4) < 3).astype(jnp.int32), jax.random.fold_in(arg_keys[1], 1), 0, 1),
    }


WATER = 0.05

def dft_tables(lag_count, freq_count):
    lag_index = jnp.arange(lag_count, dtype=jnp.int32)[:, None]
    freq_index = jnp.arange(freq_count, dtype=jnp.int32)[None, :]
    phase = (lag_index * freq_index % lag_count).astype(jnp.float32) * (2.0 * math.pi / lag_count)
    return (jnp.cos(phase).astype(jnp.bfloat16), jnp.sin(phase).astype(jnp.bfloat16))

def cross_gram(first, second):
    real_part = jnp.einsum('sfa,sfb->fab', first[0], second[0]) + jnp.einsum('sfa,sfb->fab', first[1], second[1])
    imag_part = jnp.einsum('sfa,sfb->fab', first[0], second[1]) - jnp.einsum('sfa,sfb->fab', first[1], second[0])
    return (real_part / SEG, imag_part / SEG)

def reference(spectra, seg_mask):
    tile_count = N_TILE
    half_axis = tile_count // 2
    masked = spectra * seg_mask.astype(jnp.bfloat16)[None, :, None, :]
    power = lax.optimization_barrier(jnp.sum(jnp.square(masked.astype(jnp.float32)), axis=(0, 1))) / SEG + 1e-05
    weight = power + WATER * lax.optimization_barrier(jnp.mean(power, axis=0))[None, :]
    cos_tab, sin_tab = dft_tables(LAGS, F)
    cos_wide = cos_tab.astype(jnp.float32)
    sin_wide = sin_tab.astype(jnp.float32)
    norm_scale = 1.0 / math.sqrt(LAGS)

    def one_tile(tile_idx):
        first = (tile_idx * BLK).astype(jnp.int32)
        second = ((tile_idx + half_axis) % tile_count * BLK).astype(jnp.int32)
        src_block = lax.dynamic_slice_in_dim(masked, first, BLK, 3).astype(jnp.float32)
        rcv_block = lax.dynamic_slice_in_dim(masked, second, BLK, 3).astype(jnp.float32)
        src_weight = lax.dynamic_slice_in_dim(weight, first, BLK, 1)
        rcv_weight = lax.dynamic_slice_in_dim(weight, second, BLK, 1)
        cab_re, cab_im = cross_gram(src_block, rcv_block)
        cba_re, cba_im = cross_gram(rcv_block, src_block)
        dab_re = (cab_re / src_weight[:, :, None]).astype(jnp.bfloat16).astype(jnp.float32)
        dab_im = (cab_im / src_weight[:, :, None]).astype(jnp.bfloat16).astype(jnp.float32)
        dba_re = (cba_re / rcv_weight[:, :, None]).astype(jnp.bfloat16).astype(jnp.float32)
        dba_im = (cba_im / rcv_weight[:, :, None]).astype(jnp.bfloat16).astype(jnp.float32)
        sym_re = (0.5 * (dab_re + jnp.swapaxes(dba_re, 1, 2))).astype(jnp.bfloat16)
        sym_im = (0.5 * (dab_im - jnp.swapaxes(dba_im, 1, 2))).astype(jnp.bfloat16)
        real_flat = sym_re.reshape(F, BLK * BLK).astype(jnp.float32)
        imag_flat = sym_im.reshape(F, BLK * BLK).astype(jnp.float32)
        lag_re = jnp.dot(cos_wide, real_flat, preferred_element_type=jnp.float32) - jnp.dot(sin_wide, imag_flat, preferred_element_type=jnp.float32)
        lag_im = jnp.dot(sin_wide, real_flat, preferred_element_type=jnp.float32) + jnp.dot(cos_wide, imag_flat, preferred_element_type=jnp.float32)
        energy = lag_re * lag_re + lag_im * lag_im
        mean_energy = lax.optimization_barrier(jnp.mean(energy, axis=0, keepdims=True))
        phase_part = (lag_re / jnp.sqrt(energy + 0.25 * mean_energy + 1e-05)).astype(jnp.bfloat16).astype(jnp.float32)
        out_re = jnp.dot(cos_wide.T, phase_part, preferred_element_type=jnp.float32) * norm_scale
        out_im = -jnp.dot(sin_wide.T, phase_part, preferred_element_type=jnp.float32) * norm_scale
        return jnp.stack([out_re, out_im], axis=0).astype(jnp.bfloat16).reshape(2, F, BLK, BLK)
    return lax.map(one_tile, jnp.arange(tile_count, dtype=jnp.int32))
```

```python
import math

import jax
import jax.numpy as jnp
import numpy as np
from jax import lax
from jax.experimental import pallas as pl
from jax.experimental.pallas import tpu as pltpu
from jax.sharding import PartitionSpec as P

F = 256
LAGS = 512
WATER = 0.05
STEP = 2
MESH = pl.DeviceIdType.MESH


def dft_tables(band, groups):
    lag = np.arange(LAGS)[:, None]

    def pair(freq):
        phase = (lag * freq[None, :] % LAGS).astype(np.float32) * np.float32(2.0 * math.pi / LAGS)
        return np.cos(phase.astype(np.float64)), np.sin(phase.astype(np.float64))

    chunk, src, step = np.meshgrid(
        np.arange(band // STEP), np.arange(groups), np.arange(STEP), indexing="ij"
    )
    cos_in, sin_in = pair((src * band + chunk * STEP + step).reshape(-1))
    real_rows = np.stack([cos_in, -sin_in], axis=2).reshape(LAGS, 2 * F)
    imag_rows = np.stack([sin_in, cos_in], axis=2).reshape(LAGS, 2 * F)
    cos_out, sin_out = pair(np.arange(F))
    lag_table = np.concatenate([real_rows, imag_rows], axis=0)
    out_table = np.concatenate([cos_out.T, -sin_out.T], axis=0)
    return jnp.asarray(lag_table, jnp.bfloat16), jnp.asarray(out_table, jnp.bfloat16)


def kernel(
    x_ref, mask_ref, lag_tab, out_tab, o_ref,
    wide, sent, lhs, far, sym, got, flip, rhs, spec, power, totals, inv_own, inv_far, inv_col,
    y_send, y_recv, w_sem, t_send, t_recv, z_send, z_recv,
):
    groups = lax.axis_size("freq")
    tiles = lax.axis_size("tile")
    me = lax.axis_index("freq")
    partner = {"tile": lax.rem(lax.axis_index("tile") + tiles // 2, tiles)}
    peers = [lax.rem(me + d, groups) for d in range(1, groups)]
    segs, band, block = x_ref.shape[1:]
    rows = block // groups
    chunks = band // STEP
    depth = 2 * STEP * groups

    barrier = pltpu.get_barrier_semaphore()
    for dev in [partner] + [{"freq": q} for q in peers]:
        pl.semaphore_signal(barrier, inc=1, device_id=dev, device_id_type=MESH)

    def y_copy(c):
        return pltpu.make_async_remote_copy(
            src_ref=sent.at[pl.ds(c * STEP, STEP)],
            dst_ref=far.at[pl.ds(c * STEP, STEP)],
            send_sem=y_send.at[c],
            recv_sem=y_recv.at[c],
            device_id=partner,
            device_id_type=MESH,
        )

    def z_copy(c, d):
        return pltpu.make_async_remote_copy(
            src_ref=sym.at[peers[d], pl.ds(c * STEP, STEP)],
            dst_ref=got.at[me, pl.ds(c * STEP, STEP)],
            send_sem=z_send.at[c, d],
            recv_sem=z_recv.at[c, d],
            device_id={"freq": peers[d]},
            device_id_type=MESH,
        )

    def t_copy(d):
        return pltpu.make_async_remote_copy(
            src_ref=totals.at[me],
            dst_ref=totals.at[me],
            send_sem=t_send.at[d],
            recv_sem=t_recv.at[d],
            device_id={"freq": peers[d]},
            device_id_type=MESH,
        )

    w_copy = pltpu.make_async_remote_copy(
        src_ref=inv_own,
        dst_ref=inv_far,
        send_sem=w_sem.at[0],
        recv_sem=w_sem.at[1],
        device_id=partner,
        device_id_type=MESH,
    )

    per = 8

    @pl.loop(0, segs // per)
    def _(i):
        for part in range(2):
            vals = x_ref[part, pl.ds(i * per, per)].astype(jnp.float32)
            start = pl.multiple_of((part * segs + i * per) * band, per * band)
            wide[pl.ds(start, per * band), :] = vals.reshape(per * band, block)

    mask = mask_ref[...].astype(jnp.float32)
    both = jnp.concatenate([mask, mask], axis=0)

    @pl.loop(0, band)
    def _(f):
        vals = wide[pl.ds(f, 2 * segs, stride=band), :] * both
        power[pl.ds(f, 1), :] = jnp.sum(vals * vals, axis=0, keepdims=True) / segs + 1e-05
        sent[f] = vals.astype(jnp.bfloat16)

    total = jnp.sum(power[...], axis=0, keepdims=True)
    totals[me] = jnp.broadcast_to(total, (8, block))
    pl.semaphore_wait(barrier, groups)
    for d in range(groups - 1):
        t_copy(d).start()
    for c in range(2):
        y_copy(c).start()

    @pl.loop(0, band)
    def _(f):
        turned = sent[f].astype(jnp.float32).T
        real, imag = turned[:, :segs], turned[:, segs:]
        lhs[f, :block] = turned.astype(jnp.bfloat16)
        lhs[f, block:] = jnp.concatenate([-imag, real], axis=1).astype(jnp.bfloat16)

    for d in range(groups - 1):
        t_copy(d).wait()
    whole = totals[0]
    for g in range(1, groups):
        whole = whole + totals[g]
    inv_own[...] = (1.0 / segs) / (power[...] + WATER * (whole[:1] / F))
    w_copy.start()

    @pl.loop(2, chunks)
    def _(c):
        y_copy(c).start()

    @pl.loop(0, band)
    def _(f):
        inv_col[f] = jnp.broadcast_to(inv_own[pl.ds(f, 1), :], (block, block)).T

    w_copy.wait()

    def land(c):
        for d in range(groups - 1):
            z_copy(c, d).wait()
        part = got[:, pl.ds(c * STEP, STEP)].astype(jnp.float32)
        flip[...] = part.reshape(depth * rows, block)
        for r in range(rows):
            at = pl.multiple_of(c * depth, depth)
            rhs[r, pl.ds(at, depth), :] = flip[pl.ds(r, depth, stride=rows), :].astype(jnp.bfloat16)

    def step(c):
        y_copy(c).wait()
        for i in range(STEP):
            f = c * STEP + i
            cross = jnp.dot(lhs[f], far[f], preferred_element_type=jnp.float32)
            row = inv_far[pl.ds(f, 1), :]
            col = inv_col[f]
            for part in range(2):
                vals = cross[part * block : (part + 1) * block]
                decon = (vals * col).astype(jnp.bfloat16).astype(jnp.float32)
                mirror = (vals * row).astype(jnp.bfloat16).astype(jnp.float32)
                both_sides = (0.5 * (decon + mirror)).astype(jnp.bfloat16)
                sym[:, f, part] = both_sides.reshape(groups, rows, block)
            got[me, f] = sym[me, f]
        for d in range(groups - 1):
            z_copy(c, d).start()

    lag = 2
    for c in range(lag):
        step(c)

    @pl.loop(lag, chunks)
    def _(c):
        step(c)
        land(c - lag)

    for c in range(chunks - lag, chunks):
        land(c)

    norm = 1.0 / math.sqrt(LAGS)

    @pl.loop(0, rows // 2)
    def _(i):
        pair = jnp.concatenate([rhs[2 * i], rhs[2 * i + 1]], axis=1)
        lags = jnp.dot(lag_tab[...], pair, preferred_element_type=jnp.float32)
        real, imag = lags[:LAGS], lags[LAGS:]
        energy = real * real + imag * imag
        mean = jnp.sum(energy, axis=0, keepdims=True) / LAGS
        phase = (real * lax.rsqrt(energy + (0.25 * mean + 1e-05))).astype(jnp.bfloat16)
        out = jnp.dot(out_tab[...], phase, preferred_element_type=jnp.float32) * norm
        for half in range(2):
            spec[pl.ds(2 * i + half, 2 * F, stride=rows), :] = out[:, half * block : (half + 1) * block]

    blk = 16

    @pl.loop(0, F // blk)
    def _(k):
        for part in range(2):
            at = pl.multiple_of((part * F + k * blk) * rows, blk * rows)
            vals = spec[pl.ds(at, blk * rows), :].astype(jnp.bfloat16)
            o_ref[part, pl.ds(k * blk, blk)] = vals.reshape(blk, rows, block)


def shards(spectra, seg_mask):
    groups = lax.axis_size("freq")
    _, segs, band, block = spectra.shape
    rows = block // groups
    chunks = band // STEP
    depth = 2 * STEP * groups
    lag_tab, out_tab = dft_tables(band, groups)
    vmem = pl.BlockSpec(memory_space=pltpu.VMEM)
    bf16, f32 = jnp.bfloat16, jnp.float32
    out = pl.pallas_call(
        kernel,
        out_shape=jax.ShapeDtypeStruct((2, F, rows, block), bf16),
        in_specs=[vmem] * 4,
        out_specs=vmem,
        scratch_shapes=[
            pltpu.VMEM((2 * segs * band, block), f32),
            pltpu.VMEM((band, 2 * segs, block), bf16),
            pltpu.VMEM((band, 2 * block, 2 * segs), bf16),
            pltpu.VMEM((band, 2 * segs, block), bf16),
            pltpu.VMEM((groups, band, 2, rows, block), bf16),
            pltpu.VMEM((groups, band, 2, rows, block), bf16),
            pltpu.VMEM((depth * rows, block), f32),
            pltpu.VMEM((rows, 2 * F, block), bf16),
            pltpu.VMEM((2 * F * rows, block), f32),
            pltpu.VMEM((band, block), f32),
            pltpu.VMEM((groups, 8, block), f32),
            pltpu.VMEM((band, block), f32),
            pltpu.VMEM((band, block), f32),
            pltpu.VMEM((band, block, block), f32),
            pltpu.SemaphoreType.DMA((chunks,)),
            pltpu.SemaphoreType.DMA((chunks,)),
            pltpu.SemaphoreType.DMA((2,)),
            pltpu.SemaphoreType.DMA((groups - 1,)),
            pltpu.SemaphoreType.DMA((groups - 1,)),
            pltpu.SemaphoreType.DMA((chunks, groups - 1)),
            pltpu.SemaphoreType.DMA((chunks, groups - 1)),
        ],
        compiler_params=pltpu.CompilerParams(
            collective_id=0, has_side_effects=True, vmem_limit_bytes=56 * 1024 * 1024
        ),
        name="interferometry",
    )(spectra, seg_mask, lag_tab, out_tab)
    return out[None]


def solution(mesh):
    placed = (P(None, None, "freq", "tile"), P(None, "tile"))
    return jax.shard_map(
        shards,
        mesh=mesh,
        in_specs=placed,
        out_specs=P("tile", None, None, "freq", None),
        check_vma=False,
    )
```

```python
import contextlib
import math

import jax
import jax.numpy as jnp
import numpy as np
from jax import lax
from jax.experimental import pallas as pl
from jax.experimental.pallas import tpu as pltpu
from jax.sharding import PartitionSpec as P

F = 256
LAGS = 512
HALF = LAGS // 2
WATER = 0.05
STEP = 2
AHEAD = 6
FIRST = 2
MESH = pl.DeviceIdType.MESH


def scope(name):
    return contextlib.nullcontext()


def dft_tables(band, groups):
    def pair(lag, freq):
        phase = (lag[:, None] * freq[None, :] % LAGS) * (2.0 * math.pi / LAGS)
        return np.cos(phase), np.sin(phase)

    chunk, src, step = np.meshgrid(
        np.arange(band // STEP), np.arange(groups), np.arange(STEP), indexing="ij"
    )
    order = (src * band + chunk * STEP + step).reshape(-1)
    cos_in, sin_in = pair(np.arange(HALF), order)
    sin_in[0] = pair(np.array([HALF]), order)[0][0]
    cos_out, sin_out = pair(np.arange(HALF), np.arange(F))
    lag_table = np.concatenate([cos_in, sin_in], axis=0)
    out_table = np.concatenate([cos_out.T, -sin_out.T], axis=0)
    return jnp.asarray(lag_table, jnp.bfloat16), jnp.asarray(out_table, jnp.bfloat16)


def kernel(
    x_hbm, mask_ref, lag_hbm, tab_hbm, o_ref,
    x_ref, lag_tab, out_tab, wide, sent, lhs, far, sym, got, flip, rhs, spec,
    power, totals, inv_own, inv_far, inv_col,
    in_sem, y_send, y_recv, w_sem, t_sem, z_send, z_recv, credit,
):
    groups = lax.axis_size("freq")
    tiles = lax.axis_size("tile")
    me = lax.axis_index("freq")
    partner = {"tile": lax.rem(lax.axis_index("tile") + tiles // 2, tiles)}
    ahead = {"tile": lax.rem(lax.axis_index("tile") + tiles // 4, tiles)}
    behind = {"tile": lax.rem(lax.axis_index("tile") + tiles - tiles // 4, tiles)}
    peers = [lax.rem(me + d, groups) for d in range(1, groups)]
    segs, band, block = x_ref.shape[1:]
    rows = block // groups
    chunks = band // STEP
    depth = STEP * groups

    barrier = pltpu.get_barrier_semaphore()
    for dev in [partner, ahead, behind] + [{"freq": q} for q in peers]:
        pl.semaphore_signal(barrier, inc=1, device_id=dev, device_id_type=MESH)

    def x_copy(part):
        return pltpu.make_async_copy(x_hbm.at[part], x_ref.at[part], in_sem.at[part])

    tab_copies = [
        pltpu.make_async_copy(lag_hbm, lag_tab, in_sem.at[2]),
        pltpu.make_async_copy(tab_hbm, out_tab, in_sem.at[3]),
    ]
    for part in range(2):
        x_copy(part).start()

    def y_copy(c):
        return pltpu.make_async_remote_copy(
            src_ref=sent.at[pl.ds(c * STEP, STEP)],
            dst_ref=far.at[pl.ds(c * STEP, STEP)],
            send_sem=y_send,
            recv_sem=y_recv.at[c],
            device_id=partner,
            device_id_type=MESH,
        )

    def z_copy(c, d):
        return pltpu.make_async_remote_copy(
            src_ref=sym.at[peers[d], pl.ds(c * STEP, STEP)],
            dst_ref=got.at[me, pl.ds(c * STEP, STEP)],
            send_sem=z_send,
            recv_sem=z_recv.at[c],
            device_id={"freq": peers[d]},
            device_id_type=MESH,
        )

    def t_copy(d):
        return pltpu.make_async_remote_copy(
            src_ref=totals.at[me],
            dst_ref=totals.at[me],
            send_sem=t_sem.at[0],
            recv_sem=t_sem.at[1],
            device_id={"freq": peers[d]},
            device_id_type=MESH,
        )

    def wait_bytes(ref, sem):
        pltpu.make_async_copy(ref, ref, sem).wait()

    w_copy = pltpu.make_async_remote_copy(
        src_ref=inv_own,
        dst_ref=inv_far,
        send_sem=w_sem.at[0],
        recv_sem=w_sem.at[1],
        device_id=partner,
        device_id_type=MESH,
    )

    pitch = band + 1
    per = 8
    with scope("A_convert"):
        for part in range(2):
            x_copy(part).wait()

            @pl.loop(0, segs // per)
            def _(i):
                vals = x_ref[part, pl.ds(i * per, per)].astype(jnp.float32)
                for k in range(per):
                    wide[pl.ds((part * segs + i * per + k) * pitch, band), :] = vals[k]

    for copy in tab_copies:
        copy.start()

    def lay_out(f):
        total = jnp.zeros((8, block), jnp.float32)
        for h in range(2 * segs // 16):
            vals = wide[pl.ds(f + h * 16 * pitch, 16, stride=pitch), :]
            at = h * 16 % segs
            vals = vals * mask_ref[at : at + 16].astype(jnp.float32)
            sent[f, h * 16 : (h + 1) * 16] = vals.astype(jnp.bfloat16)
            square = vals * vals
            total = total + (square[:8] + square[8:])
        power[pl.ds(f, 1), :] = jnp.sum(total, axis=0, keepdims=True) / segs + 1e-05

    with scope("B_first"):

        @pl.loop(0, FIRST * STEP)
        def _(f):
            lay_out(f)

    with scope("C_barrier"):
        pl.semaphore_wait(barrier, groups + 2)
    for c in range(FIRST):
        y_copy(c).start()

    with scope("B_rest"):

        @pl.loop(FIRST * STEP, band)
        def _(f):
            lay_out(f)

    total = jnp.sum(power[...], axis=0, keepdims=True)
    totals[me] = jnp.broadcast_to(total, (8, block))
    for d in range(groups - 1):
        t_copy(d).start()

    with scope("D_lhs"):

        @pl.loop(0, band)
        def _(f):
            turned = sent[f].astype(jnp.float32).T
            real, imag = turned[:, :segs], turned[:, segs:]
            lhs[f, :block] = turned.astype(jnp.bfloat16)
            lhs[f, block:] = jnp.concatenate([-imag, real], axis=1).astype(jnp.bfloat16)

    with scope("E_twait"):
        wait_bytes(totals.at[pl.ds(0, groups - 1)], t_sem.at[1])
        wait_bytes(totals.at[pl.ds(0, groups - 1)], t_sem.at[0])
    whole = totals[0]
    for g in range(1, groups):
        whole = whole + totals[g]
    inv_own[...] = (1.0 / segs) / (power[...] + WATER * (whole[:1] / F))
    w_copy.start()
    for c in range(FIRST, AHEAD):
        y_copy(c).start()

    @pl.loop(0, band)
    def _(f):
        inv_col[f] = jnp.broadcast_to(inv_own[pl.ds(f, 1), :], (block, block)).T

    def take(c, more):
        y_copy(c).wait_recv()
        if more:
            pl.semaphore_signal(credit, inc=1, device_id=ahead, device_id_type=MESH)
            pl.semaphore_wait(credit, 1)
            y_copy(c + AHEAD).start()

    for c in range(FIRST):
        with scope("F_take"):
            take(c, True)

    with scope("F_wwait"):
        w_copy.wait_recv()

    def land(c):
        wait_bytes(got.at[pl.ds(0, groups - 1), pl.ds(0, STEP)], z_recv.at[c])
        for src in range(groups):
            for i in range(STEP):
                for part in range(2):
                    at = (part * depth + src * STEP + i) * (rows + 1)
                    flip[at : at + rows, :] = got[src, c * STEP + i, part].astype(jnp.float32)
        for r in range(rows):
            for part in range(2):
                at = pl.multiple_of(c * depth, depth)
                vals = flip[pl.ds(part * depth * (rows + 1) + r, depth, stride=rows + 1), :]
                rhs[r, part, pl.ds(at, depth), :] = vals.astype(jnp.bfloat16)

    def step(c):
        for i in range(STEP):
            f = c * STEP + i
            cross = jnp.dot(lhs[f], far[f], preferred_element_type=jnp.float32)
            row = inv_far[pl.ds(f, 1), :]
            col = inv_col[f]
            for part in range(2):
                vals = cross[part * block : (part + 1) * block]
                decon = (vals * col).astype(jnp.bfloat16).astype(jnp.float32)
                mirror = (vals * row).astype(jnp.bfloat16).astype(jnp.float32)
                both_sides = (0.5 * (decon + mirror)).astype(jnp.bfloat16)
                sym[:, f, part] = both_sides.reshape(groups, rows, block)
            got[me, f] = sym[me, f]
        for d in range(groups - 1):
            z_copy(c, d).start()

    lag = 2
    for c in range(lag):
        with scope("G_step"):
            step(c)

    @pl.loop(lag, chunks - AHEAD)
    def _(c):
        with scope("H_take"):
            take(c, True)
        with scope("H_step"):
            step(c)
        with scope("I_land"):
            land(c - lag)

    @pl.loop(chunks - AHEAD, chunks)
    def _(c):
        with scope("H_take"):
            take(c, False)
        with scope("H_step"):
            step(c)
        with scope("I_land"):
            land(c - lag)

    for copy in tab_copies:
        copy.wait()
    for c in range(chunks - lag, chunks):
        with scope("J_land"):
            land(c)

    norm = 1.0 / math.sqrt(LAGS)
    first = lax.broadcasted_iota(jnp.int32, (8, block), 0) == 0
    odd = lax.rem(lax.broadcasted_iota(jnp.int32, (8, block), 0), 2) == 1

    def with_row0(general, special):
        return jnp.concatenate([jnp.where(first, special[:8], general[:8]), general[8:]], axis=0)

    def both_lags(r):
        pair = jnp.concatenate([rhs[r, 0], rhs[r, 1]], axis=1)
        prod = jnp.dot(lag_tab[...], pair, preferred_element_type=jnp.float32)
        cos_re, cos_im = prod[:HALF, :block], prod[:HALF, block:]
        sin_re, sin_im = prod[HALF:, :block], prod[HALF:, block:]
        up_re = with_row0(cos_re - sin_im, cos_re)
        up_im = with_row0(cos_im + sin_re, cos_im)
        down_re = with_row0(cos_re + sin_im, sin_re)
        down_im = with_row0(cos_im - sin_re, sin_im)
        up = up_re * up_re + up_im * up_im
        down = down_re * down_re + down_im * down_im
        mean = jnp.sum(up + down, axis=0, keepdims=True) / LAGS
        base = 0.25 * mean + 1e-05
        up_norm = up_re * lax.rsqrt(up + base)
        down_norm = down_re * lax.rsqrt(down + base)
        middle = down_norm[:1]
        even = with_row0(up_norm + down_norm, up_norm).astype(jnp.bfloat16)
        return even, (up_norm - down_norm).astype(jnp.bfloat16), middle

    with scope("K_transform"):

        @pl.loop(0, rows // 2)
        def _(i):
            even0, odd0, mid0 = both_lags(2 * i)
            even1, odd1, mid1 = both_lags(2 * i + 1)
            even = jnp.concatenate([even0, even1], axis=1)
            odds = jnp.concatenate([odd0, odd1], axis=1)
            re = jnp.dot(out_tab[:F], even, preferred_element_type=jnp.float32)
            im = jnp.dot(out_tab[F:], odds, preferred_element_type=jnp.float32)
            for half, mid in ((0, mid0), (1, mid1)):
                cols = slice(half * block, (half + 1) * block)
                signed = jnp.where(odd, -mid, mid)
                signed = jnp.broadcast_to(signed[None], (F // 8, 8, block)).reshape(F, block)
                at = (2 * i + half) * (2 * F + 1)
                spec[pl.ds(at, F), :] = (re[:, cols] + signed) * norm
                spec[pl.ds(at + F, F), :] = im[:, cols] * norm

    blk = 8
    with scope("L_conv"):

        @pl.loop(0, F // blk)
        def _(k):
            for part in range(2):
                for i in range(blk):
                    at = part * F + k * blk + i
                    vals = spec[pl.ds(at, rows, stride=2 * F + 1), :]
                    o_ref[part, k * blk + i] = vals.astype(jnp.bfloat16)

    with scope("M_drain"):
        w_copy.wait_send()
        wait_bytes(sent, y_send)
        wait_bytes(sym.at[pl.ds(0, groups - 1)], z_send)


def shards(spectra, seg_mask):
    groups = lax.axis_size("freq")
    _, segs, band, block = spectra.shape
    rows = block // groups
    chunks = band // STEP
    depth = STEP * groups
    lag_tab, out_tab = dft_tables(band, groups)
    vmem = pl.BlockSpec(memory_space=pltpu.VMEM)
    hbm = pl.BlockSpec(memory_space=pltpu.HBM)
    bf16, f32 = jnp.bfloat16, jnp.float32
    out = pl.pallas_call(
        kernel,
        out_shape=jax.ShapeDtypeStruct((2, F, rows, block), bf16),
        in_specs=[hbm, vmem, hbm, hbm],
        out_specs=vmem,
        scratch_shapes=[
            pltpu.VMEM(spectra.shape, bf16),
            pltpu.VMEM(lag_tab.shape, bf16),
            pltpu.VMEM(out_tab.shape, bf16),
            pltpu.VMEM((2 * segs * (band + 1), block), f32),
            pltpu.VMEM((band, 2 * segs, block), bf16),
            pltpu.VMEM((band, 2 * block, 2 * segs), bf16),
            pltpu.VMEM((band, 2 * segs, block), bf16),
            pltpu.VMEM((groups, band, 2, rows, block), bf16),
            pltpu.VMEM((groups, band, 2, rows, block), bf16),
            pltpu.VMEM((2 * depth * (rows + 1), block), f32),
            pltpu.VMEM((rows, 2, F, block), bf16),
            pltpu.VMEM((rows * (2 * F + 1) + 8, block), f32),
            pltpu.VMEM((band, block), f32),
            pltpu.VMEM((groups, 8, block), f32),
            pltpu.VMEM((band, block), f32),
            pltpu.VMEM((band, block), f32),
            pltpu.VMEM((band, block, block), f32),
            pltpu.SemaphoreType.DMA((4,)),
            pltpu.SemaphoreType.DMA,
            pltpu.SemaphoreType.DMA((chunks,)),
            pltpu.SemaphoreType.DMA((2,)),
            pltpu.SemaphoreType.DMA((2,)),
            pltpu.SemaphoreType.DMA,
            pltpu.SemaphoreType.DMA((chunks,)),
            pltpu.SemaphoreType.REGULAR,
        ],
        compiler_params=pltpu.CompilerParams(
            collective_id=0, has_side_effects=True, vmem_limit_bytes=40 * 1024 * 1024
        ),
        name="interferometry",
    )(*(pltpu.with_memory_space_constraint(a, pltpu.HBM) for a in (spectra, seg_mask, lag_tab, out_tab)))
    return out[None]


def solution(mesh):
    placed = (P(None, None, "freq", "tile"), P(None, "tile"))
    return jax.shard_map(
        shards,
        mesh=mesh,
        in_specs=placed,
        out_specs=P("tile", None, None, "freq", None),
        check_vma=False,
    )
```

```python
import contextlib
import math

import jax
import jax.numpy as jnp
import numpy as np
from jax import lax
from jax.experimental import pallas as pl
from jax.experimental.pallas import tpu as pltpu
from jax.sharding import PartitionSpec as P

F = 256
LAGS = 512
HALF = LAGS // 2
WATER = 0.05
STEP = 2
AHEAD = 4
BEHIND = 5
FIRST = 2
MESH = pl.DeviceIdType.MESH


def scope(name):
    return contextlib.nullcontext()


def dft_tables(band, groups):
    def pair(lag, freq):
        phase = (lag[:, None] * freq[None, :] % LAGS) * (2.0 * math.pi / LAGS)
        return np.cos(phase), np.sin(phase)

    chunk, src, step = np.meshgrid(
        np.arange(band // STEP), np.arange(groups), np.arange(STEP), indexing="ij"
    )
    order = (src * band + chunk * STEP + step).reshape(-1)
    cos_in, sin_in = pair(np.arange(HALF), order)
    sin_in[0] = pair(np.array([HALF]), order)[0][0]
    cos_out, sin_out = pair(np.arange(HALF), np.arange(F))
    lag_table = np.concatenate([cos_in, sin_in], axis=0)
    out_table = np.concatenate([cos_out.T, -sin_out.T], axis=0)
    return jnp.asarray(lag_table, jnp.bfloat16), jnp.asarray(out_table, jnp.bfloat16)


def kernel(
    x_hbm, mask_hbm, lag_hbm, tab_hbm, o_ref,
    x_ref, mask_ref, lag_tab, out_tab, wide, sent, lhs, far, sym, got, flip, rhs, spec,
    prod0, prod1, prod2, prod3, power, totals, own_total, far_total, inv_own, inv_col,
    in_sem, y_send, y_recv, w_sem, t_sem, z_send, z_recv, credit,
):
    groups = lax.axis_size("freq")
    tiles = lax.axis_size("tile")
    me = lax.axis_index("freq")
    partner = {"tile": lax.rem(lax.axis_index("tile") + tiles // 2, tiles)}
    ahead = {"tile": lax.rem(lax.axis_index("tile") + tiles // 4, tiles)}
    behind = {"tile": lax.rem(lax.axis_index("tile") + tiles - tiles // 4, tiles)}
    peers = [lax.rem(me + d, groups) for d in range(1, groups)]
    segs, band, block = x_ref.shape[1:]
    rows = block // groups
    chunks = band // STEP
    depth = STEP * groups

    def x_copy(part):
        return pltpu.make_async_copy(x_hbm.at[part], x_ref.at[part], in_sem.at[part])

    tab_copies = [
        pltpu.make_async_copy(lag_hbm, lag_tab, in_sem.at[2]),
        pltpu.make_async_copy(tab_hbm, out_tab, in_sem.at[3]),
    ]
    mask_copy = pltpu.make_async_copy(mask_hbm, mask_ref, in_sem.at[4])

    barrier = pltpu.get_barrier_semaphore()
    for part in range(2):
        x_copy(part).start()
    mask_copy.start()
    for dev in [partner, ahead, behind] + [{"freq": q} for q in peers]:
        pl.semaphore_signal(barrier, inc=1, device_id=dev, device_id_type=MESH)

    def y_copy(c, first=None, count=STEP):
        part = pl.ds(c * STEP if first is None else first, count)
        return pltpu.make_async_remote_copy(
            src_ref=sent.at[part],
            dst_ref=far.at[part],
            send_sem=y_send,
            recv_sem=y_recv.at[c],
            device_id=partner,
            device_id_type=MESH,
        )

    def z_copy(c, d, first=None, count=STEP):
        part = pl.ds(c * STEP if first is None else first, count)
        return pltpu.make_async_remote_copy(
            src_ref=sym.at[peers[d], part],
            dst_ref=got.at[me, part],
            send_sem=z_send,
            recv_sem=z_recv.at[c],
            device_id={"freq": peers[d]},
            device_id_type=MESH,
        )

    last = [(chunks - 1 + i, band - STEP + i, 1) for i in range(STEP)]

    def t_copy(d):
        return pltpu.make_async_remote_copy(
            src_ref=totals.at[me],
            dst_ref=totals.at[me],
            send_sem=t_sem.at[0],
            recv_sem=t_sem.at[1],
            device_id={"freq": peers[d]},
            device_id_type=MESH,
        )

    def wait_bytes(ref, sem):
        pltpu.make_async_copy(ref, ref, sem).wait()

    w_copy = pltpu.make_async_remote_copy(
        src_ref=own_total,
        dst_ref=far_total,
        send_sem=w_sem.at[0],
        recv_sem=w_sem.at[1],
        device_id=partner,
        device_id_type=MESH,
    )

    pitch = band + 1
    per = 8
    with scope("A_convert"):
        for part in range(2):
            x_copy(part).wait()

            @pl.loop(0, segs // per)
            def _(i):
                vals = x_ref[part, pl.ds(i * per, per)].astype(jnp.float32)
                for k in range(per):
                    wide[pl.ds((part * segs + i * per + k) * pitch, band), :] = vals[k]

    for copy in tab_copies:
        copy.start()
    mask_copy.wait()

    def mean_square(vals):
        squares = [v * v for v in vals]
        while len(squares) > 1:
            squares = [a + b for a, b in zip(squares[::2], squares[1::2])]
        return jnp.sum(squares[0], axis=0, keepdims=True) / segs + 1e-05

    def lay_out(f):
        parts = []
        for h in range(2 * segs // 16):
            vals = wide[pl.ds(f + h * 16 * pitch, 16, stride=pitch), :]
            at = h * 16 % segs
            vals = vals * mask_ref[at : at + 16].astype(jnp.float32)
            sent[f, h * 16 : (h + 1) * 16] = vals.astype(jnp.bfloat16)
            parts += [vals[:8], vals[8:]]
        power[pl.ds(f, 1), :] = mean_square(parts)

    with scope("B_first"):

        @pl.loop(0, FIRST * STEP)
        def _(f):
            lay_out(f)

    with scope("C_barrier"):
        pl.semaphore_wait(barrier, groups + 2)
    for c in range(FIRST):
        y_copy(c).start()

    with scope("B_rest"):

        @pl.loop(FIRST * STEP, band)
        def _(f):
            lay_out(f)

    total = jnp.sum(power[...], axis=0, keepdims=True)
    totals[me] = jnp.broadcast_to(total, (8, block))
    for d in range(groups - 1):
        t_copy(d).start()

    with scope("D_lhs"):

        @pl.loop(0, band)
        def _(f):
            turned = sent[f].astype(jnp.float32).T
            real, imag = turned[:, :segs], turned[:, segs:]
            lhs[f, :block] = turned.astype(jnp.bfloat16)
            lhs[f, block:] = jnp.concatenate([-imag, real], axis=1).astype(jnp.bfloat16)

    with scope("E_twait"):
        wait_bytes(totals.at[pl.ds(0, groups - 1)], t_sem.at[1])
        wait_bytes(totals.at[pl.ds(0, groups - 1)], t_sem.at[0])
    whole = totals[0]
    for g in range(1, groups):
        whole = whole + totals[g]
    own_total[...] = whole
    w_copy.start()
    for c in range(FIRST, AHEAD):
        y_copy(c).start()

    def inverse(power_row, total_row):
        return (1.0 / segs) / (power_row + WATER * (total_row / F))

    inv_own[...] = inverse(power[...], own_total[:1])

    @pl.loop(0, band)
    def _(f):
        inv_col[f] = jnp.broadcast_to(inv_own[pl.ds(f, 1), :], (block, block)).T

    def take(c, more=True):
        y_copy(c).wait_recv()
        if more:
            pl.semaphore_signal(credit, inc=1, device_id=ahead, device_id_type=MESH)
            pl.semaphore_wait(credit, 1)
            if isinstance(c, int) and c + AHEAD == chunks - 1:
                for piece in last:
                    y_copy(*piece).start()
            else:
                y_copy(c + AHEAD).start()

    for c in range(FIRST):
        with scope("F_take"):
            take(c)

    with scope("F_wwait"):
        w_copy.wait_recv()

    def land(c):
        if isinstance(c, int) and c == chunks - 1:
            for sem, _, count in last:
                wait_bytes(got.at[pl.ds(0, groups - 1), pl.ds(0, count)], z_recv.at[sem])
        else:
            wait_bytes(got.at[pl.ds(0, groups - 1), pl.ds(0, STEP)], z_recv.at[c])
        for src in range(groups):
            for i in range(STEP):
                for part in range(2):
                    at = (part * depth + src * STEP + i) * (rows + 1)
                    flip[at : at + rows, :] = got[src, c * STEP + i, part].astype(jnp.float32)
        for r in range(rows):
            for part in range(2):
                at = pl.multiple_of(c * depth, depth)
                vals = flip[pl.ds(part * depth * (rows + 1) + r, depth, stride=rows + 1), :]
                rhs[r, part, pl.ds(at, depth), :] = vals.astype(jnp.bfloat16)

    def symmetric(f):
        cross = jnp.dot(lhs[f], far[f], preferred_element_type=jnp.float32)
        vals = far[f].astype(jnp.float32)
        row = inverse(mean_square([vals[k : k + 8] for k in range(0, 2 * segs, 8)]), far_total[:1])
        col = inv_col[f]
        for part in range(2):
            vals = cross[part * block : (part + 1) * block]
            decon = (vals * col).astype(jnp.bfloat16).astype(jnp.float32)
            mirror = (vals * row).astype(jnp.bfloat16).astype(jnp.float32)
            both_sides = (0.5 * (decon + mirror)).astype(jnp.bfloat16)
            sym[:, f, part] = both_sides.reshape(groups, rows, block)
        got[me, f] = sym[me, f]

    def step(c):
        for i in range(STEP):
            symmetric(c * STEP + i)
        for d in range(groups - 1):
            z_copy(c, d).start()

    with scope("G_step"):
        for c in range(FIRST):
            step(c)

    def round_of(c, more):
        with scope("H_take"):
            take(c, more)
        with scope("H_step"):
            step(c)

    def round_and_land(c, more):
        round_of(c, more)
        with scope("I_land"):
            land(c - BEHIND)

    @pl.loop(FIRST, BEHIND)
    def _(c):
        round_of(c, True)

    @pl.loop(BEHIND, chunks - AHEAD - 1)
    def _(c):
        round_and_land(c, True)

    round_and_land(chunks - AHEAD - 1, True)

    @pl.loop(chunks - AHEAD, chunks - 1)
    def _(c):
        round_and_land(c, False)

    for sem, f, count in last:
        with scope("H_take"):
            y_copy(sem, f, count).wait_recv()
        with scope("H_step"):
            symmetric(f)
            for d in range(groups - 1):
                z_copy(sem, d, f, count).start()

    for copy in tab_copies:
        copy.wait()

    @pl.loop(chunks - 1 - BEHIND, chunks - 1)
    def _(c):
        with scope("J_land"):
            land(c)

    with scope("J_last"):
        land(chunks - 1)

    prod = [prod0, prod1, prod2, prod3]
    norm = 1.0 / math.sqrt(LAGS)
    first = lax.broadcasted_iota(jnp.int32, (8, block), 0) == 0
    odd = lax.rem(lax.broadcasted_iota(jnp.int32, (8, block), 0), 2) == 1

    def with_row0(general, special):
        return jnp.concatenate([jnp.where(first, special[:8], general[:8]), general[8:]], axis=0)

    def products(r, out):
        pair = jnp.concatenate([rhs[r, 0], rhs[r, 1]], axis=1)
        out[...] = jnp.dot(lag_tab[...], pair, preferred_element_type=jnp.float32)

    def both_lags(prod):
        cos_re, cos_im = prod[:HALF, :block], prod[:HALF, block:]
        sin_re, sin_im = prod[HALF:, :block], prod[HALF:, block:]
        up_re = with_row0(cos_re - sin_im, cos_re)
        up_im = with_row0(cos_im + sin_re, cos_im)
        down_re = with_row0(cos_re + sin_im, sin_re)
        down_im = with_row0(cos_im - sin_re, sin_im)
        up = up_re * up_re + up_im * up_im
        down = down_re * down_re + down_im * down_im
        mean = jnp.sum(up + down, axis=0, keepdims=True) / LAGS
        base = 0.25 * mean + 1e-05
        up_norm = up_re * lax.rsqrt(up + base)
        down_norm = down_re * lax.rsqrt(down + base)
        middle = down_norm[:1]
        even = with_row0(up_norm + down_norm, up_norm).astype(jnp.bfloat16)
        return even, (up_norm - down_norm).astype(jnp.bfloat16), middle

    with scope("K_transform"):

        def spectrum(r, prods):
            even0, odd0, mid0 = both_lags(prods[0])
            even1, odd1, mid1 = both_lags(prods[1])
            even = jnp.concatenate([even0, even1], axis=1)
            odds = jnp.concatenate([odd0, odd1], axis=1)
            re = jnp.dot(out_tab[:F], even, preferred_element_type=jnp.float32)
            im = jnp.dot(out_tab[F:], odds, preferred_element_type=jnp.float32)
            for half, mid in ((0, mid0), (1, mid1)):
                cols = slice(half * block, (half + 1) * block)
                signed = jnp.where(odd, -mid, mid)
                signed = jnp.broadcast_to(signed[None], (F // 8, 8, block)).reshape(F, block)
                at = (r + half) * (2 * F + 1)
                spec[pl.ds(at, F), :] = re[:, cols] + signed
                spec[pl.ds(at + F, F), :] = im[:, cols]

        for k in range(2):
            products(k, prod[k])

        @pl.loop(0, rows // 4)
        def _(i):
            for k in range(2):
                r = 4 * i + 2 * k
                ready = prod[2 * k : 2 * k + 2]
                for m in range(2):
                    products(lax.rem(r + 2 + m, rows), prod[2 - 2 * k + m])
                spectrum(r, ready)

    blk = 8
    with scope("L_conv"):

        @pl.loop(0, F // blk)
        def _(k):
            for part in range(2):
                for i in range(blk):
                    at = part * F + k * blk + i
                    vals = spec[pl.ds(at, rows, stride=2 * F + 1), :]
                    o_ref[part, k * blk + i] = (vals * norm).astype(jnp.bfloat16)

    with scope("M_drain"):
        w_copy.wait_send()
        wait_bytes(sent, y_send)
        wait_bytes(sym.at[pl.ds(0, groups - 1)], z_send)


def shards(spectra, seg_mask):
    groups = lax.axis_size("freq")
    _, segs, band, block = spectra.shape
    rows = block // groups
    chunks = band // STEP
    depth = STEP * groups
    lag_tab, out_tab = dft_tables(band, groups)
    vmem = pl.BlockSpec(memory_space=pltpu.VMEM)
    hbm = pl.BlockSpec(memory_space=pltpu.HBM)
    bf16, f32 = jnp.bfloat16, jnp.float32
    out = pl.pallas_call(
        kernel,
        out_shape=jax.ShapeDtypeStruct((2, F, rows, block), bf16),
        in_specs=[hbm] * 4,
        out_specs=vmem,
        scratch_shapes=[
            pltpu.VMEM(spectra.shape, bf16),
            pltpu.VMEM(seg_mask.shape, seg_mask.dtype),
            pltpu.VMEM(lag_tab.shape, bf16),
            pltpu.VMEM(out_tab.shape, bf16),
            pltpu.VMEM((2 * segs * (band + 1), block), f32),
            pltpu.VMEM((band, 2 * segs, block), bf16),
            pltpu.VMEM((band, 2 * block, 2 * segs), bf16),
            pltpu.VMEM((band, 2 * segs, block), bf16),
            pltpu.VMEM((groups, band, 2, rows, block), bf16),
            pltpu.VMEM((groups, band, 2, rows, block), bf16),
            pltpu.VMEM((2 * depth * (rows + 1), block), f32),
            pltpu.VMEM((rows, 2, F, block), bf16),
            pltpu.VMEM((rows * (2 * F + 1) + 8, block), f32),
            *[pltpu.VMEM((2 * HALF, 2 * block), f32)] * 4,
            pltpu.VMEM((band, block), f32),
            pltpu.VMEM((groups, 8, block), f32),
            pltpu.VMEM((8, block), f32),
            pltpu.VMEM((8, block), f32),
            pltpu.VMEM((band, block), f32),
            pltpu.VMEM((band, block, block), f32),
            pltpu.SemaphoreType.DMA((5,)),
            pltpu.SemaphoreType.DMA,
            pltpu.SemaphoreType.DMA((chunks + STEP - 1,)),
            pltpu.SemaphoreType.DMA((2,)),
            pltpu.SemaphoreType.DMA((2,)),
            pltpu.SemaphoreType.DMA,
            pltpu.SemaphoreType.DMA((chunks + STEP - 1,)),
            pltpu.SemaphoreType.REGULAR,
        ],
        compiler_params=pltpu.CompilerParams(
            collective_id=0, has_side_effects=True, vmem_limit_bytes=40 * 1024 * 1024
        ),
        name="interferometry",
    )(*(pltpu.with_memory_space_constraint(a, pltpu.HBM) for a in (spectra, seg_mask, lag_tab, out_tab)))
    return out[None]


def solution(mesh):
    placed = (P(None, None, "freq", "tile"), P(None, "tile"))
    return jax.shard_map(
        shards,
        mesh=mesh,
        in_specs=placed,
        out_specs=P("tile", None, None, "freq", None),
        check_vma=False,
    )
```

```python
import contextlib
import math

import jax
import jax.numpy as jnp
import numpy as np
from jax import lax
from jax.experimental import pallas as pl
from jax.experimental.pallas import tpu as pltpu
from jax.sharding import PartitionSpec as P

F = 256
LAGS = 512
HALF = LAGS // 2
WATER = 0.05
STEP = 2
AHEAD = 5
TAIL = 5
BEHIND = 5
FIRST = 2
MESH = pl.DeviceIdType.MESH


def scope(name):
    return contextlib.nullcontext()


def dft_tables(band, groups):
    def pair(lag, freq):
        phase = (lag[:, None] * freq[None, :] % LAGS) * (2.0 * math.pi / LAGS)
        return np.cos(phase), np.sin(phase)

    chunk, src, step = np.meshgrid(
        np.arange(band // STEP), np.arange(groups), np.arange(STEP), indexing="ij"
    )
    order = (src * band + chunk * STEP + step).reshape(-1)
    cos_in, sin_in = pair(np.arange(HALF), order)
    sin_in[0] = pair(np.array([HALF]), order)[0][0]
    cos_out, sin_out = pair(np.arange(HALF), np.arange(F))
    lag_table = np.concatenate([cos_in, sin_in], axis=0)
    out_table = np.concatenate([cos_out.T, -sin_out.T], axis=0)
    return jnp.asarray(lag_table, jnp.bfloat16), jnp.asarray(out_table, jnp.bfloat16)


def kernel(
    x_hbm, mask_hbm, lag_hbm, tab_hbm, o_ref,
    x_ref, mask_ref, lag_tab, out_tab, wide, sent, lhs, far, sym, got, flip, rhs, spec,
    prod0, prod1, prod2, prod3, energy, power, totals, own_total, far_total, inv_own, inv_col,
    in_sem, y_send, y_recv, w_sem, t_sem, z_send, z_recv, credit,
):
    groups = lax.axis_size("freq")
    tiles = lax.axis_size("tile")
    me = lax.axis_index("freq")
    partner = {"tile": lax.rem(lax.axis_index("tile") + tiles // 2, tiles)}
    ahead = {"tile": lax.rem(lax.axis_index("tile") + tiles // 4, tiles)}
    behind = {"tile": lax.rem(lax.axis_index("tile") + tiles - tiles // 4, tiles)}
    peers = [lax.rem(me + d, groups) for d in range(1, groups)]
    segs, band, block = x_ref.shape[1:]
    rows = block // groups
    chunks = band // STEP
    depth = STEP * groups

    def x_copy(part):
        return pltpu.make_async_copy(x_hbm.at[part], x_ref.at[part], in_sem.at[part])

    tab_copies = [
        pltpu.make_async_copy(lag_hbm, lag_tab, in_sem.at[2]),
        pltpu.make_async_copy(tab_hbm, out_tab, in_sem.at[3]),
    ]
    mask_copy = pltpu.make_async_copy(mask_hbm, mask_ref, in_sem.at[4])

    barrier = pltpu.get_barrier_semaphore()
    for part in range(2):
        x_copy(part).start()
    mask_copy.start()
    for dev in [partner, ahead, behind] + [{"freq": q} for q in peers]:
        pl.semaphore_signal(barrier, inc=1, device_id=dev, device_id_type=MESH)

    def y_copy(c, first=None, count=STEP):
        part = pl.ds(c * STEP if first is None else first, count)
        return pltpu.make_async_remote_copy(
            src_ref=sent.at[part],
            dst_ref=far.at[part],
            send_sem=y_send,
            recv_sem=y_recv.at[c],
            device_id=partner,
            device_id_type=MESH,
        )

    def z_copy(c, d, first=None, count=STEP):
        part = pl.ds(c * STEP if first is None else first, count)
        return pltpu.make_async_remote_copy(
            src_ref=sym.at[peers[d], part],
            dst_ref=got.at[me, part],
            send_sem=z_send,
            recv_sem=z_recv.at[c],
            device_id={"freq": peers[d]},
            device_id_type=MESH,
        )

    last = [(chunks - 1 + i, band - STEP + i, 1) for i in range(STEP)]

    def t_copy(d):
        return pltpu.make_async_remote_copy(
            src_ref=totals.at[me],
            dst_ref=totals.at[me],
            send_sem=t_sem.at[0],
            recv_sem=t_sem.at[1],
            device_id={"freq": peers[d]},
            device_id_type=MESH,
        )

    def wait_bytes(ref, sem):
        pltpu.make_async_copy(ref, ref, sem).wait()

    w_copy = pltpu.make_async_remote_copy(
        src_ref=own_total,
        dst_ref=far_total,
        send_sem=w_sem.at[0],
        recv_sem=w_sem.at[1],
        device_id=partner,
        device_id_type=MESH,
    )

    pitch = band + 1
    per = 8
    with scope("A_convert"):
        for part in range(2):
            x_copy(part).wait()

            @pl.loop(0, segs // per)
            def _(i):
                vals = x_ref[part, pl.ds(i * per, per)].astype(jnp.float32)
                for k in range(per):
                    wide[pl.ds((part * segs + i * per + k) * pitch, band), :] = vals[k]

    for copy in tab_copies:
        copy.start()
    mask_copy.wait()

    def mean_square(vals):
        squares = [v * v for v in vals]
        while len(squares) > 1:
            squares = [a + b for a, b in zip(squares[::2], squares[1::2])]
        return jnp.sum(squares[0], axis=0, keepdims=True) / segs + 1e-05

    def lay_out(f):
        parts = []
        for h in range(2 * segs // 16):
            vals = wide[pl.ds(f + h * 16 * pitch, 16, stride=pitch), :]
            at = h * 16 % segs
            vals = vals * mask_ref[at : at + 16].astype(jnp.float32)
            sent[f, h * 16 : (h + 1) * 16] = vals.astype(jnp.bfloat16)
            parts += [vals[:8], vals[8:]]
        power[pl.ds(f, 1), :] = mean_square(parts)

    with scope("B_first"):

        @pl.loop(0, FIRST * STEP)
        def _(f):
            lay_out(f)

    with scope("C_barrier"):
        pl.semaphore_wait(barrier, groups + 2)
    for c in range(FIRST):
        y_copy(c).start()

    with scope("B_rest"):

        @pl.loop(FIRST * STEP, band)
        def _(f):
            lay_out(f)

    total = jnp.sum(power[...], axis=0, keepdims=True)
    totals[me] = jnp.broadcast_to(total, (8, block))
    for d in range(groups - 1):
        t_copy(d).start()

    with scope("D_lhs"):

        @pl.loop(0, band)
        def _(f):
            turned = sent[f].astype(jnp.float32).T
            real, imag = turned[:, :segs], turned[:, segs:]
            lhs[f, :block] = turned.astype(jnp.bfloat16)
            lhs[f, block:] = jnp.concatenate([-imag, real], axis=1).astype(jnp.bfloat16)

    with scope("E_twait"):
        wait_bytes(totals.at[pl.ds(0, groups - 1)], t_sem.at[1])
        wait_bytes(totals.at[pl.ds(0, groups - 1)], t_sem.at[0])
    whole = totals[0]
    for g in range(1, groups):
        whole = whole + totals[g]
    own_total[...] = whole
    w_copy.start()
    energy[...] = jnp.zeros_like(energy)
    for c in range(FIRST, AHEAD):
        y_copy(c).start()

    def inverse(power_row, total_row):
        return (1.0 / segs) / (power_row + WATER * (total_row / F))

    inv_own[...] = inverse(power[...], own_total[:1])

    @pl.loop(0, band)
    def _(f):
        inv_col[f] = jnp.broadcast_to(inv_own[pl.ds(f, 1), :], (block, block)).T

    def take(c, more=True):
        y_copy(c).wait_recv()
        if more:
            pl.semaphore_signal(credit, inc=1, device_id=ahead, device_id_type=MESH)
            pl.semaphore_wait(credit, 1)
            if more is True:
                y_copy(c + AHEAD).start()
            else:
                y_copy(*more).start()

    for c in range(FIRST):
        with scope("F_take"):
            take(c)

    with scope("F_wwait"):
        w_copy.wait_recv()

    def land(c):
        if isinstance(c, int) and c == chunks - 1:
            for sem, _, count in last:
                wait_bytes(got.at[pl.ds(0, groups - 1), pl.ds(0, count)], z_recv.at[sem])
        else:
            wait_bytes(got.at[pl.ds(0, groups - 1), pl.ds(0, STEP)], z_recv.at[c])
        squares = [jnp.zeros((rows, block), jnp.float32)] * 2
        for src in range(groups):
            for i in range(STEP):
                for part in range(2):
                    at = (part * depth + src * STEP + i) * (rows + 1)
                    vals = got[src, c * STEP + i, part].astype(jnp.float32)
                    flip[at : at + rows, :] = vals
                    squares[part] = squares[part] + vals * vals
        energy[...] += squares[0] + squares[1]
        for r in range(rows):
            for part in range(2):
                at = pl.multiple_of(c * depth, depth)
                vals = flip[pl.ds(part * depth * (rows + 1) + r, depth, stride=rows + 1), :]
                rhs[r, part, pl.ds(at, depth), :] = vals.astype(jnp.bfloat16)

    def symmetric(f):
        cross = jnp.dot(lhs[f], far[f], preferred_element_type=jnp.float32)
        vals = far[f].astype(jnp.float32)
        row = inverse(mean_square([vals[k : k + 8] for k in range(0, 2 * segs, 8)]), far_total[:1])
        col = inv_col[f]
        for part in range(2):
            vals = cross[part * block : (part + 1) * block]
            decon = (vals * col).astype(jnp.bfloat16).astype(jnp.float32)
            mirror = (vals * row).astype(jnp.bfloat16).astype(jnp.float32)
            both_sides = (0.5 * (decon + mirror)).astype(jnp.bfloat16)
            sym[:, f, part] = both_sides.reshape(groups, rows, block)
        got[me, f] = sym[me, f]

    def step(c):
        for i in range(STEP):
            symmetric(c * STEP + i)
        for d in range(groups - 1):
            z_copy(c, d).start()

    with scope("G_step"):
        for c in range(FIRST):
            step(c)

    def round_of(c, more):
        with scope("H_take"):
            take(c, more)
        with scope("H_step"):
            step(c)

    def round_and_land(c, more):
        round_of(c, more)
        with scope("I_land"):
            land(c - BEHIND)

    @pl.loop(FIRST, BEHIND)
    def _(c):
        round_of(c, True)

    @pl.loop(BEHIND, chunks - AHEAD - 1)
    def _(c):
        round_and_land(c, True)

    hold = dict(zip(range(chunks - TAIL, chunks - TAIL + STEP), last))
    for c in range(chunks - AHEAD - 1, chunks - 1):
        round_and_land(c, hold.get(c, False))

    for sem, f, count in last:
        with scope("H_take"):
            y_copy(sem, f, count).wait_recv()
        with scope("H_step"):
            symmetric(f)
            for d in range(groups - 1):
                z_copy(sem, d, f, count).start()

    for copy in tab_copies:
        copy.wait()

    @pl.loop(chunks - 1 - BEHIND, chunks - 1)
    def _(c):
        with scope("J_land"):
            land(c)

    with scope("J_last"):
        land(chunks - 1)

    prod = [prod0, prod1, prod2, prod3]
    norm = 1.0 / math.sqrt(LAGS)
    first = lax.broadcasted_iota(jnp.int32, (8, block), 0) == 0
    odd = lax.rem(lax.broadcasted_iota(jnp.int32, (8, block), 0), 2) == 1

    def with_row0(general, special):
        return jnp.concatenate([jnp.where(first, special[:8], general[:8]), general[8:]], axis=0)

    def products(r, out):
        pair = jnp.concatenate([rhs[r, 0], rhs[r, 1]], axis=1)
        out[...] = jnp.dot(lag_tab[...], pair, preferred_element_type=jnp.float32)

    def both_lags(r, prod):
        base = 0.25 * energy[pl.ds(r, 1), :] + 1e-05
        evens, odds = [], []
        for b in range(0, HALF, 32):
            cos_re, cos_im = prod[b : b + 32, :block], prod[b : b + 32, block:]
            at = HALF + b
            sin_re, sin_im = prod[at : at + 32, :block], prod[at : at + 32, block:]
            up_re, up_im = cos_re - sin_im, cos_im + sin_re
            down_re, down_im = cos_re + sin_im, cos_im - sin_re
            if b == 0:
                up_re, up_im = with_row0(up_re, cos_re), with_row0(up_im, cos_im)
                down_re, down_im = with_row0(down_re, sin_re), with_row0(down_im, sin_im)
            up_norm = up_re * lax.rsqrt(up_re * up_re + up_im * up_im + base)
            down_norm = down_re * lax.rsqrt(down_re * down_re + down_im * down_im + base)
            even = up_norm + down_norm
            if b == 0:
                middle = down_norm[:1]
                even = with_row0(even, up_norm)
            evens.append(even.astype(jnp.bfloat16))
            odds.append((up_norm - down_norm).astype(jnp.bfloat16))
        return jnp.concatenate(evens, axis=0), jnp.concatenate(odds, axis=0), middle

    with scope("K_transform"):

        def spectrum(r, prods):
            even0, odd0, mid0 = both_lags(r, prods[0])
            even1, odd1, mid1 = both_lags(r + 1, prods[1])
            even = jnp.concatenate([even0, even1], axis=1)
            odds = jnp.concatenate([odd0, odd1], axis=1)
            re = jnp.dot(out_tab[:F], even, preferred_element_type=jnp.float32)
            im = jnp.dot(out_tab[F:], odds, preferred_element_type=jnp.float32)
            for half, mid in ((0, mid0), (1, mid1)):
                cols = slice(half * block, (half + 1) * block)
                signed = jnp.where(odd, -mid, mid)
                signed = jnp.broadcast_to(signed[None], (F // 8, 8, block)).reshape(F, block)
                at = (r + half) * (2 * F + 1)
                spec[pl.ds(at, F), :] = re[:, cols] + signed
                spec[pl.ds(at + F, F), :] = im[:, cols]

        for k in range(2):
            products(k, prod[k])

        @pl.loop(0, rows // 4)
        def _(i):
            for k in range(2):
                r = 4 * i + 2 * k
                ready = prod[2 * k : 2 * k + 2]
                for m in range(2):
                    products(lax.rem(r + 2 + m, rows), prod[2 - 2 * k + m])
                spectrum(r, ready)

    blk = 8
    with scope("L_conv"):

        @pl.loop(0, F // blk)
        def _(k):
            for part in range(2):
                for i in range(blk):
                    at = part * F + k * blk + i
                    vals = spec[pl.ds(at, rows, stride=2 * F + 1), :]
                    o_ref[part, k * blk + i] = (vals * norm).astype(jnp.bfloat16)

    with scope("M_drain"):
        w_copy.wait_send()
        wait_bytes(sent, y_send)
        wait_bytes(sym.at[pl.ds(0, groups - 1)], z_send)


def shards(spectra, seg_mask):
    groups = lax.axis_size("freq")
    _, segs, band, block = spectra.shape
    rows = block // groups
    chunks = band // STEP
    depth = STEP * groups
    lag_tab, out_tab = dft_tables(band, groups)
    vmem = pl.BlockSpec(memory_space=pltpu.VMEM)
    hbm = pl.BlockSpec(memory_space=pltpu.HBM)
    bf16, f32 = jnp.bfloat16, jnp.float32
    out = pl.pallas_call(
        kernel,
        out_shape=jax.ShapeDtypeStruct((2, F, rows, block), bf16),
        in_specs=[hbm] * 4,
        out_specs=vmem,
        scratch_shapes=[
            pltpu.VMEM(spectra.shape, bf16),
            pltpu.VMEM(seg_mask.shape, seg_mask.dtype),
            pltpu.VMEM(lag_tab.shape, bf16),
            pltpu.VMEM(out_tab.shape, bf16),
            pltpu.VMEM((2 * segs * (band + 1), block), f32),
            pltpu.VMEM((band, 2 * segs, block), bf16),
            pltpu.VMEM((band, 2 * block, 2 * segs), bf16),
            pltpu.VMEM((band, 2 * segs, block), bf16),
            pltpu.VMEM((groups, band, 2, rows, block), bf16),
            pltpu.VMEM((groups, band, 2, rows, block), bf16),
            pltpu.VMEM((2 * depth * (rows + 1), block), f32),
            pltpu.VMEM((rows, 2, F, block), bf16),
            pltpu.VMEM((rows * (2 * F + 1) + 8, block), f32),
            *[pltpu.VMEM((2 * HALF, 2 * block), f32)] * 4,
            pltpu.VMEM((rows, block), f32),
            pltpu.VMEM((band, block), f32),
            pltpu.VMEM((groups, 8, block), f32),
            pltpu.VMEM((8, block), f32),
            pltpu.VMEM((8, block), f32),
            pltpu.VMEM((band, block), f32),
            pltpu.VMEM((band, block, block), f32),
            pltpu.SemaphoreType.DMA((5,)),
            pltpu.SemaphoreType.DMA,
            pltpu.SemaphoreType.DMA((chunks + STEP - 1,)),
            pltpu.SemaphoreType.DMA((2,)),
            pltpu.SemaphoreType.DMA((2,)),
            pltpu.SemaphoreType.DMA,
            pltpu.SemaphoreType.DMA((chunks + STEP - 1,)),
            pltpu.SemaphoreType.REGULAR,
        ],
        compiler_params=pltpu.CompilerParams(
            collective_id=0, has_side_effects=True, vmem_limit_bytes=40 * 1024 * 1024
        ),
        name="interferometry",
    )(*(pltpu.with_memory_space_constraint(a, pltpu.HBM) for a in (spectra, seg_mask, lag_tab, out_tab)))
    return out[None]


def solution(mesh):
    placed = (P(None, None, "freq", "tile"), P(None, "tile"))
    return jax.shard_map(
        shards,
        mesh=mesh,
        in_specs=placed,
        out_specs=P("tile", None, None, "freq", None),
        check_vma=False,
    )
```

```python
import contextlib
import math

import jax
import jax.numpy as jnp
import numpy as np
from jax import lax
from jax.experimental import pallas as pl
from jax.experimental.pallas import tpu as pltpu
from jax.sharding import PartitionSpec as P

F = 256
LAGS = 512
HALF = LAGS // 2
WATER = 0.05
STEP = 2
AHEAD = 5
TAIL = 5
BEHIND = 5
FIRST = 2
MESH = pl.DeviceIdType.MESH


def scope(name):
    return contextlib.nullcontext()


def dft_tables(band, groups):
    def pair(lag, freq):
        phase = (lag[:, None] * freq[None, :] % LAGS) * (2.0 * math.pi / LAGS)
        return np.cos(phase), np.sin(phase)

    chunk, src, step = np.meshgrid(
        np.arange(band // STEP), np.arange(groups), np.arange(STEP), indexing="ij"
    )
    order = (src * band + chunk * STEP + step).reshape(-1)
    cos_in, sin_in = pair(np.arange(HALF), order)
    sin_in[0] = pair(np.array([HALF]), order)[0][0]
    cos_out, sin_out = pair(np.arange(HALF), np.arange(F))
    lag_table = np.concatenate([cos_in, sin_in], axis=0)
    out_table = np.concatenate([cos_out.T, -sin_out.T], axis=0)
    return jnp.asarray(lag_table, jnp.bfloat16), jnp.asarray(out_table, jnp.bfloat16)


def kernel(
    x_hbm, mask_hbm, lag_hbm, tab_hbm, o_ref,
    x_ref, mask_ref, lag_tab, out_tab, wide, sent, lhs, far, sym, got, flip, rhs, spec,
    prod0, prod1, prod2, prod3, energy, power, totals, own_total, far_total, inv_own, inv_col,
    in_sem, y_send, y_recv, w_sem, t_sem, z_send, z_recv, credit,
):
    groups = lax.axis_size("freq")
    tiles = lax.axis_size("tile")
    me = lax.axis_index("freq")
    partner = {"tile": lax.rem(lax.axis_index("tile") + tiles // 2, tiles)}
    ahead = {"tile": lax.rem(lax.axis_index("tile") + tiles // 4, tiles)}
    behind = {"tile": lax.rem(lax.axis_index("tile") + tiles - tiles // 4, tiles)}
    order = sorted(range(1, groups), key=lambda d: abs(d - groups // 2))
    peers = [lax.rem(me + d, groups) for d in order]
    segs, band, block = x_ref.shape[1:]
    rows = block // groups
    chunks = band // STEP
    depth = STEP * groups

    def x_copy(part):
        return pltpu.make_async_copy(x_hbm.at[part], x_ref.at[part], in_sem.at[part])

    tab_copies = [
        pltpu.make_async_copy(lag_hbm, lag_tab, in_sem.at[2]),
        pltpu.make_async_copy(tab_hbm, out_tab, in_sem.at[3]),
    ]
    mask_copy = pltpu.make_async_copy(mask_hbm, mask_ref, in_sem.at[4])

    barrier = pltpu.get_barrier_semaphore()
    for part in range(2):
        x_copy(part).start()
    mask_copy.start()
    for dev in [partner, ahead, behind] + [{"freq": q} for q in peers]:
        pl.semaphore_signal(barrier, inc=1, device_id=dev, device_id_type=MESH)

    def y_copy(c, first=None, count=STEP):
        part = pl.ds(c * STEP if first is None else first, count)
        return pltpu.make_async_remote_copy(
            src_ref=sent.at[part],
            dst_ref=far.at[part],
            send_sem=y_send,
            recv_sem=y_recv.at[c],
            device_id=partner,
            device_id_type=MESH,
        )

    def z_copy(c, d, first=None, count=STEP):
        part = pl.ds(c * STEP if first is None else first, count)
        return pltpu.make_async_remote_copy(
            src_ref=sym.at[peers[d], part],
            dst_ref=got.at[me, part],
            send_sem=z_send,
            recv_sem=z_recv.at[c],
            device_id={"freq": peers[d]},
            device_id_type=MESH,
        )

    last = [(chunks - 1 + i, band - STEP + i, 1) for i in range(STEP)]

    def t_copy(d):
        return pltpu.make_async_remote_copy(
            src_ref=totals.at[me],
            dst_ref=totals.at[me],
            send_sem=t_sem.at[0],
            recv_sem=t_sem.at[1],
            device_id={"freq": peers[d]},
            device_id_type=MESH,
        )

    def wait_bytes(ref, sem):
        pltpu.make_async_copy(ref, ref, sem).wait()

    w_copy = pltpu.make_async_remote_copy(
        src_ref=own_total,
        dst_ref=far_total,
        send_sem=w_sem.at[0],
        recv_sem=w_sem.at[1],
        device_id=partner,
        device_id_type=MESH,
    )

    pitch = band + 1
    per = 8
    with scope("A_convert"):
        for part in range(2):
            x_copy(part).wait()

            @pl.loop(0, segs // per)
            def _(i):
                vals = x_ref[part, pl.ds(i * per, per)].astype(jnp.float32)
                for k in range(per):
                    wide[pl.ds((part * segs + i * per + k) * pitch, band), :] = vals[k]

    for copy in tab_copies:
        copy.start()
    mask_copy.wait()

    def mean_square(vals):
        squares = [v * v for v in vals]
        while len(squares) > 1:
            squares = [a + b for a, b in zip(squares[::2], squares[1::2])]
        return jnp.sum(squares[0], axis=0, keepdims=True) / segs + 1e-05

    def lay_out(f):
        parts = []
        for h in range(2 * segs // 16):
            vals = wide[pl.ds(f + h * 16 * pitch, 16, stride=pitch), :]
            at = h * 16 % segs
            vals = vals * mask_ref[at : at + 16].astype(jnp.float32)
            sent[f, h * 16 : (h + 1) * 16] = vals.astype(jnp.bfloat16)
            parts += [vals[:8], vals[8:]]
        power[pl.ds(f, 1), :] = mean_square(parts)

    with scope("B_first"):

        @pl.loop(0, FIRST * STEP)
        def _(f):
            lay_out(f)

    with scope("C_barrier"):
        pl.semaphore_wait(barrier, groups + 2)
    for c in range(FIRST):
        y_copy(c).start()

    with scope("B_rest"):

        @pl.loop(FIRST * STEP, band)
        def _(f):
            lay_out(f)

    total = jnp.sum(power[...], axis=0, keepdims=True)
    totals[me] = jnp.broadcast_to(total, (8, block))
    for d in range(groups - 1):
        t_copy(d).start()

    with scope("D_lhs"):

        @pl.loop(0, band)
        def _(f):
            turned = sent[f].astype(jnp.float32).T
            real, imag = turned[:, :segs], turned[:, segs:]
            lhs[f, :block] = turned.astype(jnp.bfloat16)
            lhs[f, block:] = jnp.concatenate([-imag, real], axis=1).astype(jnp.bfloat16)

    with scope("E_twait"):
        wait_bytes(totals.at[pl.ds(0, groups - 1)], t_sem.at[1])
        wait_bytes(totals.at[pl.ds(0, groups - 1)], t_sem.at[0])
    whole = totals[0]
    for g in range(1, groups):
        whole = whole + totals[g]
    own_total[...] = whole
    w_copy.start()
    energy[...] = jnp.zeros_like(energy)
    for c in range(FIRST, AHEAD):
        y_copy(c).start()

    def inverse(power_row, total_row):
        return (1.0 / segs) / (power_row + WATER * (total_row / F))

    inv_own[...] = inverse(power[...], own_total[:1])

    @pl.loop(0, band)
    def _(f):
        inv_col[f] = jnp.broadcast_to(inv_own[pl.ds(f, 1), :], (block, block)).T

    def take(c, more=True):
        y_copy(c).wait_recv()
        if more:
            pl.semaphore_signal(credit, inc=1, device_id=ahead, device_id_type=MESH)
            pl.semaphore_wait(credit, 1)
            if more is True:
                y_copy(c + AHEAD).start()
            else:
                y_copy(*more).start()

    for c in range(FIRST):
        with scope("F_take"):
            take(c)

    with scope("F_wwait"):
        w_copy.wait_recv()

    def land(c):
        if isinstance(c, int) and c == chunks - 1:
            for sem, _, count in last:
                wait_bytes(got.at[pl.ds(0, groups - 1), pl.ds(0, count)], z_recv.at[sem])
        else:
            wait_bytes(got.at[pl.ds(0, groups - 1), pl.ds(0, STEP)], z_recv.at[c])
        squares = [jnp.zeros((rows, block), jnp.float32)] * 2
        for src in range(groups):
            for i in range(STEP):
                for part in range(2):
                    at = (part * depth + src * STEP + i) * (rows + 1)
                    vals = got[src, c * STEP + i, part].astype(jnp.float32)
                    flip[at : at + rows, :] = vals
                    squares[part] = squares[part] + vals * vals
        energy[...] += squares[0] + squares[1]
        for r in range(rows):
            for part in range(2):
                at = pl.multiple_of(c * depth, depth)
                vals = flip[pl.ds(part * depth * (rows + 1) + r, depth, stride=rows + 1), :]
                rhs[r, part, pl.ds(at, depth), :] = vals.astype(jnp.bfloat16)

    def symmetric(f):
        cross = jnp.dot(lhs[f], far[f], preferred_element_type=jnp.float32)
        vals = far[f].astype(jnp.float32)
        row = inverse(mean_square([vals[k : k + 8] for k in range(0, 2 * segs, 8)]), far_total[:1])
        col = inv_col[f]
        for part in range(2):
            vals = cross[part * block : (part + 1) * block]
            decon = (vals * col).astype(jnp.bfloat16).astype(jnp.float32)
            mirror = (vals * row).astype(jnp.bfloat16).astype(jnp.float32)
            both_sides = (0.5 * (decon + mirror)).astype(jnp.bfloat16)
            sym[:, f, part] = both_sides.reshape(groups, rows, block)
        got[me, f] = sym[me, f]

    def step(c):
        for i in range(STEP):
            symmetric(c * STEP + i)
        for d in range(groups - 1):
            z_copy(c, d).start()

    with scope("G_step"):
        for c in range(FIRST):
            step(c)

    def round_of(c, more):
        with scope("H_take"):
            take(c, more)
        with scope("H_step"):
            step(c)

    def round_and_land(c, more):
        round_of(c, more)
        with scope("I_land"):
            land(c - BEHIND)

    @pl.loop(FIRST, BEHIND)
    def _(c):
        round_of(c, True)

    @pl.loop(BEHIND, chunks - AHEAD - 1)
    def _(c):
        round_and_land(c, True)

    hold = dict(zip(range(chunks - TAIL, chunks - TAIL + STEP), last))
    for c in range(chunks - AHEAD - 1, chunks - 1):
        round_and_land(c, hold.get(c, False))

    for sem, f, count in last:
        with scope("H_take"):
            y_copy(sem, f, count).wait_recv()
        with scope("H_step"):
            symmetric(f)
            for d in range(groups - 1):
                z_copy(sem, d, f, count).start()

    for copy in tab_copies:
        copy.wait()

    @pl.loop(chunks - 1 - BEHIND, chunks - 1)
    def _(c):
        with scope("J_land"):
            land(c)

    with scope("J_last"):
        land(chunks - 1)

    prod = [prod0, prod1, prod2, prod3]
    norm = 1.0 / math.sqrt(LAGS)
    first = lax.broadcasted_iota(jnp.int32, (8, block), 0) == 0
    odd = lax.rem(lax.broadcasted_iota(jnp.int32, (8, block), 0), 2) == 1

    def with_row0(general, special):
        return jnp.concatenate([jnp.where(first, special[:8], general[:8]), general[8:]], axis=0)

    def products(r, out):
        pair = jnp.concatenate([rhs[r, 0], rhs[r, 1]], axis=1)
        out[...] = jnp.dot(lag_tab[...], pair, preferred_element_type=jnp.float32)

    def both_lags(r, prod):
        base = 0.25 * energy[pl.ds(r, 1), :] + 1e-05
        evens, odds = [], []
        for b in range(0, HALF, 32):
            cos_re, cos_im = prod[b : b + 32, :block], prod[b : b + 32, block:]
            at = HALF + b
            sin_re, sin_im = prod[at : at + 32, :block], prod[at : at + 32, block:]
            up_re, up_im = cos_re - sin_im, cos_im + sin_re
            down_re, down_im = cos_re + sin_im, cos_im - sin_re
            if b == 0:
                up_re, up_im = with_row0(up_re, cos_re), with_row0(up_im, cos_im)
                down_re, down_im = with_row0(down_re, sin_re), with_row0(down_im, sin_im)
            up_norm = up_re * lax.rsqrt(up_re * up_re + up_im * up_im + base)
            down_norm = down_re * lax.rsqrt(down_re * down_re + down_im * down_im + base)
            even = up_norm + down_norm
            if b == 0:
                middle = down_norm[:1]
                even = with_row0(even, up_norm)
            evens.append(even.astype(jnp.bfloat16))
            odds.append((up_norm - down_norm).astype(jnp.bfloat16))
        return jnp.concatenate(evens, axis=0), jnp.concatenate(odds, axis=0), middle

    with scope("K_transform"):

        def spectrum(r, prods):
            even0, odd0, mid0 = both_lags(r, prods[0])
            even1, odd1, mid1 = both_lags(r + 1, prods[1])
            even = jnp.concatenate([even0, even1], axis=1)
            odds = jnp.concatenate([odd0, odd1], axis=1)
            re = jnp.dot(out_tab[:F], even, preferred_element_type=jnp.float32)
            im = jnp.dot(out_tab[F:], odds, preferred_element_type=jnp.float32)
            for half, mid in ((0, mid0), (1, mid1)):
                cols = slice(half * block, (half + 1) * block)
                signed = jnp.where(odd, -mid, mid)
                signed = jnp.broadcast_to(signed[None], (F // 8, 8, block)).reshape(F, block)
                at = (r + half) * (2 * F + 1)
                spec[pl.ds(at, F), :] = re[:, cols] + signed
                spec[pl.ds(at + F, F), :] = im[:, cols]

        for k in range(2):
            products(k, prod[k])

        @pl.loop(0, rows // 4)
        def _(i):
            for k in range(2):
                r = 4 * i + 2 * k
                ready = prod[2 * k : 2 * k + 2]
                for m in range(2):
                    products(lax.rem(r + 2 + m, rows), prod[2 - 2 * k + m])
                spectrum(r, ready)

    blk = 8
    with scope("L_conv"):

        @pl.loop(0, F // blk)
        def _(k):
            for part in range(2):
                for i in range(blk):
                    at = part * F + k * blk + i
                    vals = spec[pl.ds(at, rows, stride=2 * F + 1), :]
                    o_ref[part, k * blk + i] = (vals * norm).astype(jnp.bfloat16)

    with scope("M_drain"):
        w_copy.wait_send()
        wait_bytes(sent, y_send)
        wait_bytes(sym.at[pl.ds(0, groups - 1)], z_send)


def shards(spectra, seg_mask):
    groups = lax.axis_size("freq")
    _, segs, band, block = spectra.shape
    rows = block // groups
    chunks = band // STEP
    depth = STEP * groups
    lag_tab, out_tab = dft_tables(band, groups)
    vmem = pl.BlockSpec(memory_space=pltpu.VMEM)
    hbm = pl.BlockSpec(memory_space=pltpu.HBM)
    bf16, f32 = jnp.bfloat16, jnp.float32
    out = pl.pallas_call(
        kernel,
        out_shape=jax.ShapeDtypeStruct((2, F, rows, block), bf16),
        in_specs=[hbm] * 4,
        out_specs=vmem,
        scratch_shapes=[
            pltpu.VMEM(spectra.shape, bf16),
            pltpu.VMEM(seg_mask.shape, seg_mask.dtype),
            pltpu.VMEM(lag_tab.shape, bf16),
            pltpu.VMEM(out_tab.shape, bf16),
            pltpu.VMEM((2 * segs * (band + 1), block), f32),
            pltpu.VMEM((band, 2 * segs, block), bf16),
            pltpu.VMEM((band, 2 * block, 2 * segs), bf16),
            pltpu.VMEM((band, 2 * segs, block), bf16),
            pltpu.VMEM((groups, band, 2, rows, block), bf16),
            pltpu.VMEM((groups, band, 2, rows, block), bf16),
            pltpu.VMEM((2 * depth * (rows + 1), block), f32),
            pltpu.VMEM((rows, 2, F, block), bf16),
            pltpu.VMEM((rows * (2 * F + 1) + 8, block), f32),
            *[pltpu.VMEM((2 * HALF, 2 * block), f32)] * 4,
            pltpu.VMEM((rows, block), f32),
            pltpu.VMEM((band, block), f32),
            pltpu.VMEM((groups, 8, block), f32),
            pltpu.VMEM((8, block), f32),
            pltpu.VMEM((8, block), f32),
            pltpu.VMEM((band, block), f32),
            pltpu.VMEM((band, block, block), f32),
            pltpu.SemaphoreType.DMA((5,)),
            pltpu.SemaphoreType.DMA,
            pltpu.SemaphoreType.DMA((chunks + STEP - 1,)),
            pltpu.SemaphoreType.DMA((2,)),
            pltpu.SemaphoreType.DMA((2,)),
            pltpu.SemaphoreType.DMA,
            pltpu.SemaphoreType.DMA((chunks + STEP - 1,)),
            pltpu.SemaphoreType.REGULAR,
        ],
        compiler_params=pltpu.CompilerParams(
            collective_id=0, has_side_effects=True, vmem_limit_bytes=40 * 1024 * 1024
        ),
        name="interferometry",
    )(*(pltpu.with_memory_space_constraint(a, pltpu.HBM) for a in (spectra, seg_mask, lag_tab, out_tab)))
    return out[None]


def solution(mesh):
    placed = (P(None, None, "freq", "tile"), P(None, "tile"))
    return jax.shard_map(
        shards,
        mesh=mesh,
        in_specs=placed,
        out_specs=P("tile", None, None, "freq", None),
        check_vma=False,
    )
```
